32 devices in a mesh: dp: 4 (over z), row: 4 (over y, core), col: 2 (over x).
Axes of the slice: x: 2, y: 2, z: 4, core: 2. Of those that a mesh axis runs over, the one named last changes fastest.
Arguments:
- block_in: float32 [4, 1024, 1024], P('dp', 'row', 'col'), may hold values from -37 to 37
- out_grad: float32 [4, 1024, 1024], P('dp', 'row', 'col'), may hold values from -6 to 6
- segment_ids: int32 [4, 1024], P('dp'), may hold values from 0 to 2, never falling along the last dimension, each value on 1 to 512 neighbouring positions
- attn_gain: float32 [1024], P('col'), may hold values from 0.5 to 1.5
- w_query: bfloat16 [1024, 1024], P('col', 'row'), may hold values from -0.125 to 0.125
- w_key: bfloat16 [1024, 512], P('col', 'row'), may hold values from -0.125 to 0.125
- w_value: bfloat16 [1024, 512], P('col', 'row'), may hold values from -0.1875 to 0.1875
- query_gain: float32 [64], replicated, may hold values from 0.5 to 5.5
- key_gain: float32 [64], replicated, may hold values from 0.5 to 5.5
- w_out: bfloat16 [1024, 1024], P('row', 'col'), may hold values from -1.5 to 1.5
- ffn_gain: float32 [1024], P('col'), may hold values from 0.5 to 1.5
- w_gate: bfloat16 [1024, 4608], P('col', 'row'), may hold values from -0.1875 to 0.1875
- w_up: bfloat16 [1024, 4608], P('col', 'row'), may hold values from -0.1875 to 0.1875
- w_down: bfloat16 [4608, 1024], P('row', 'col'), may hold values from -0.09375 to 0.09375
Outputs:
- block_out: float32 [4, 1024, 1024], P('dp', 'row', 'col')
- in_grad: float32 [4, 1024, 1024], P('dp', 'row', 'col')
- grad_attn_gain: float32 [1024], P('col')
- grad_query: float32 [1024, 1024], P('col', 'row')
- grad_key: float32 [1024, 512], P('col', 'row')
- grad_value: float32 [1024, 512], P('col', 'row')
- grad_query_gain: float32 [64], replicated
- grad_key_gain: float32 [64], replicated
- grad_out: float32 [1024, 1024], P('row', 'col')
- grad_ffn_gain: float32 [1024], P('col')
- grad_gate: float32 [1024, 4608], P('col', 'row')
- grad_up: float32 [1024, 4608], P('col', 'row')
- grad_down: float32 [4608, 1024], P('row', 'col')
The draws below stay inside these ranges and needn't reach their ends.
Inputs may be any that keep to these rules, and one draw needn't show every extreme that they name: `segment_ids`: in each sequence the numbers never fall along the positions; each document holds 1 to 512 tokens and some document holds exactly 512.
All inputs are finite; a program needn't handle non-finite values.
Results may differ from the reference program's by a relative error of at most 0.028.
The reference program's roundings to bfloat16 on the way count: a program that leaves them out, or rounds other values in their place, can miss the bound.
Values may be sent and summed in bfloat16 or wider, within the bound.
No kernel may reach another device: no remote copies, remote signals or barrier semaphores. Data moves between devices by JAX's collectives and lax.ppermute only.
A program may use at most 128 MiB of HBM per device.

```python
import math
import jax
import jax.numpy as jnp
import numpy as np
from jax import lax

D = 1024
HEADS = 16
KV_HEADS = 8
HEAD = 64
FF = 4608
SEQ = 1024
BATCH = 4
DOCS = 3
DOC_MOST = 512


def query_base(key):
    return jax.random.truncated_normal(jax.random.fold_in(key, 101), -4.0, 4.0, (D, HEADS * HEAD), jnp.float32) * D ** (-0.5)


def draw_w_query(key, part):
    return query_base(key).astype(jnp.bfloat16)


def draw_w_key(key, part):
    fresh = jax.random.truncated_normal(jax.random.fold_in(key, 102), -4.0, 4.0, (D, KV_HEADS * HEAD), jnp.float32) * D ** (-0.5)
    return fresh.astype(jnp.bfloat16)


def draw_query_gain(key, part):
    return jax.random.uniform(jax.random.fold_in(key, 301), (HEAD,), jnp.float32, 0.5, 1.5)


def draw_key_gain(key, part):
    return jax.random.uniform(jax.random.fold_in(key, 302), (HEAD,), jnp.float32, 0.5, 1.5)


def draw_block_in(key, part):
    row_scales = jnp.exp(jax.random.uniform(jax.random.fold_in(key, 202), (BATCH, SEQ, 1), jnp.float32, math.log(0.3), math.log(3.0)))
    col_scales = jnp.exp(jax.random.uniform(jax.random.fold_in(key, 203), (1, 1, D), jnp.float32, math.log(0.3), math.log(3.0)))
    base = jax.random.truncated_normal(jax.random.fold_in(key, 201), -4.0, 4.0, (BATCH, SEQ, D), jnp.float32)
    return base * row_scales * col_scales


def levels(key, dims, cuts, smallest, high):
    level = 1.0
    for dim, shards_of in cuts:
        heights = jax.random.uniform(jax.random.fold_in(jax.random.fold_in(key, 6), dim), (shards_of,), jnp.float32, smallest / len(cuts), high / len(cuts))
        level = level * jnp.repeat(jnp.exp(heights), dims[dim] // shards_of).reshape((-1,) + (1,) * (len(dims) - 1 - dim))
    return level


def length_profile(number_of, total, bound, lean):
    loads = [(1 << 20) // math.isqrt(rank ** lean) + 1 for rank in range(2, number_of + 1)]
    surplus, holding = total - bound - (number_of - 1), [1] * (number_of - 1)
    while surplus > 0:
        movable = [i for i in range(number_of - 1) if holding[i] < bound]
        mass, remaining = sum([loads[i] for i in movable]), surplus
        for i in movable:
            addition = min(bound - holding[i], max(1, remaining * loads[i] // mass), surplus)
            holding[i] = holding[i] + addition
            surplus = surplus - addition
    return np.array([bound] + holding)


def uneven(stream_key, number_of, total, limit, slope):
    if number_of == 2:
        one = jax.random.randint(stream_key, (), max(1, total - limit), min(limit, total - 1) + 1)
        return jnp.stack([one, total - one])
    lengths = jnp.asarray(length_profile(number_of, total, limit, slope), jnp.int32)
    pairs = (number_of - 1) // 2
    giver, taker = lengths[1:1 + 2 * pairs:2], lengths[2:2 + 2 * pairs:2]
    slack = jnp.minimum(giver - 1, limit - taker)
    moved = jax.random.randint(jax.random.fold_in(stream_key, 1), (pairs,), 0, 1 << 20) % (slack + 1)
    lengths = lengths.at[1:1 + 2 * pairs:2].set(giver - moved).at[2:2 + 2 * pairs:2].set(taker + moved)
    return lengths[jax.random.permutation(jax.random.fold_in(stream_key, 2), number_of)]


def noise(stream_key, extent, scale, bound, split=(), held_as=jnp.bfloat16):
    loudness = levels(stream_key, extent, split, -0.22, 0.18) if split else 1.0
    array = jax.random.normal(stream_key, extent, jnp.float32) * scale * loudness
    return jnp.minimum(jnp.maximum(array, -bound), bound).astype(held_as)


def setup_inputs(seed: int = 0) -> dict:
    key_of = jax.random.split(jax.random.key(seed), 15)
    block_in = draw_block_in(jax.random.fold_in(key_of[14], 71), 0)
    out_grad = noise(key_of[1], (BATCH, SEQ, D), 1.0, 6.0, ((0, 4), (1, 4), (2, 2)), jnp.float32)
    segment_ids = jax.vmap(lambda own: jnp.searchsorted(jnp.cumsum(uneven(own, DOCS, SEQ, DOC_MOST, 1)), jnp.arange(SEQ), side="right"))(jax.random.split(key_of[2], BATCH)).reshape((BATCH, SEQ)).astype(jnp.int32)
    attn_gain = jnp.clip(1.0 + 0.1 * jax.random.normal(key_of[3], (D,), jnp.float32), 0.5, 1.5)
    w_query = draw_w_query(jax.random.fold_in(key_of[14], 71), 0)
    w_key = draw_w_key(jax.random.fold_in(key_of[14], 71), 0)
    w_value = noise(key_of[6], (D, KV_HEADS * HEAD), D ** -0.5, 0.1875, ((0, 2), (1, 4)))
    query_gain = draw_query_gain(jax.random.fold_in(key_of[14], 71), 0)
    key_gain = draw_key_gain(jax.random.fold_in(key_of[14], 71), 0)
    w_out = noise(key_of[9], (HEADS * HEAD, D), (max(16, HEADS * HEAD // 64)) ** -0.5, 1.5, ((0, 4), (1, 2)))
    ffn_gain = jnp.clip(1.0 + 0.1 * jax.random.normal(key_of[10], (D,), jnp.float32), 0.5, 1.5)
    w_gate = noise(key_of[11], (D, FF), D ** -0.5, 0.1875, ((0, 2), (1, 4)))
    w_up = noise(key_of[12], (D, FF), D ** -0.5, 0.1875, ((0, 2), (1, 4)))
    w_down = noise(key_of[13], (FF, D), FF ** -0.5, 0.09375, ((0, 4), (1, 2)))
    return dict(block_in=block_in, out_grad=out_grad, segment_ids=segment_ids, attn_gain=attn_gain, w_query=w_query, w_key=w_key, w_value=w_value, query_gain=query_gain, key_gain=key_gain, w_out=w_out, ffn_gain=ffn_gain, w_gate=w_gate, w_up=w_up, w_down=w_down)


NORM_EPSILON = 1e-05
ROPE_BASE = 1000000.0

def rope_tables(length, head_width):
    half_width = head_width // 2
    exponents = jnp.arange(half_width, dtype=jnp.float32) * (2.0 / head_width)
    frequency = ROPE_BASE ** (-exponents)
    angles = jnp.arange(length, dtype=jnp.float32)[:, None] * frequency[None, :]
    return (jnp.cos(angles), jnp.sin(angles))

def rotate(vectors, cosine, sine, direction):
    half_width = vectors.shape[-1] // 2
    first_half = vectors[..., :half_width]
    second_half = vectors[..., half_width:]
    cos_rows = cosine[:, None, :]
    sin_rows = sine[:, None, :] * direction
    return jnp.concatenate([first_half * cos_rows - second_half * sin_rows, second_half * cos_rows + first_half * sin_rows], axis=-1)

def rounded(values):
    return lax.optimization_barrier(values.astype(jnp.bfloat16))

def norm_back(grad_rows, unit_rows, scale_rows, gain):
    weighted = grad_rows * gain
    return scale_rows * (weighted - unit_rows * lax.optimization_barrier(jnp.mean(weighted * unit_rows, axis=-1, keepdims=True)))

def one_sequence(stream, upstream, segments, attn_gain, w_query, w_key, w_value, query_gain, key_gain, w_out, ffn_gain, w_gate, w_up, w_down):
    length = stream.shape[0]
    group_size = HEADS // KV_HEADS
    score_scale = HEAD ** (-0.5)
    cosine, sine = rope_tables(length, HEAD)
    scale_one = lax.rsqrt(lax.optimization_barrier(jnp.mean(stream * stream, axis=1, keepdims=True)) + NORM_EPSILON)
    unit_one = stream * scale_one
    normed_one = rounded(unit_one * attn_gain)
    query_rows = jnp.dot(normed_one, w_query, preferred_element_type=jnp.float32).reshape(length, HEADS, HEAD)
    key_rows = jnp.dot(normed_one, w_key, preferred_element_type=jnp.float32).reshape(length, KV_HEADS, HEAD)
    value_rows = jnp.dot(normed_one, w_value, preferred_element_type=jnp.float32).reshape(length, KV_HEADS, HEAD)
    q_scale = lax.rsqrt(lax.optimization_barrier(jnp.mean(query_rows * query_rows, axis=-1, keepdims=True)) + NORM_EPSILON)
    q_unit = query_rows * q_scale
    k_scale = lax.rsqrt(lax.optimization_barrier(jnp.mean(key_rows * key_rows, axis=-1, keepdims=True)) + NORM_EPSILON)
    k_unit = key_rows * k_scale
    q_rot = rounded(rotate(q_unit * query_gain, cosine, sine, 1.0)).astype(jnp.float32)
    k_rot = rounded(rotate(k_unit * key_gain, cosine, sine, 1.0)).astype(jnp.float32)
    v_rows = rounded(value_rows).astype(jnp.float32)
    k_wide = jnp.repeat(k_rot, group_size, axis=1)
    v_wide = jnp.repeat(v_rows, group_size, axis=1)
    positions = jnp.arange(length)
    allowed = (segments[:, None] == segments[None, :]) & (positions[:, None] >= positions[None, :])
    scores = jnp.einsum('qhd,khd->hqk', q_rot, k_wide) * score_scale
    scores = jnp.where(allowed[None], scores, -jnp.inf)
    row_top = lax.optimization_barrier(jnp.max(scores, axis=-1, keepdims=True))
    log_total = row_top + jnp.log(lax.optimization_barrier(jnp.sum(jnp.exp(scores - row_top), axis=-1, keepdims=True)))
    attn_probs = jnp.exp(scores - log_total)
    probs_b = rounded(attn_probs).astype(jnp.float32)
    attn_rows = jnp.einsum('hqk,khd->qhd', probs_b, v_wide)
    attn_b = rounded(attn_rows.reshape(length, HEADS * HEAD))
    middle = stream + jnp.dot(attn_b, w_out, preferred_element_type=jnp.float32)
    scale_two = lax.rsqrt(lax.optimization_barrier(jnp.mean(middle * middle, axis=1, keepdims=True)) + NORM_EPSILON)
    unit_two = middle * scale_two
    normed_two = rounded(unit_two * ffn_gain)
    gate = jnp.dot(normed_two, w_gate, preferred_element_type=jnp.float32)
    up_proj = jnp.dot(normed_two, w_up, preferred_element_type=jnp.float32)
    sigmoid_gate = jax.nn.sigmoid(gate)
    silu_gate = gate * sigmoid_gate
    activated = rounded(silu_gate * up_proj)
    block_out = middle + jnp.dot(activated, w_down, preferred_element_type=jnp.float32)
    grad_b = rounded(upstream)
    d_act = jnp.dot(grad_b, w_down.T, preferred_element_type=jnp.float32)
    grad_down = jnp.dot(activated.T, grad_b, preferred_element_type=jnp.float32)
    d_gate = rounded(d_act * up_proj * (sigmoid_gate * (1.0 + gate * (1.0 - sigmoid_gate))))
    d_up = rounded(d_act * silu_gate)
    grad_gate = jnp.dot(normed_two.T, d_gate, preferred_element_type=jnp.float32)
    grad_up = jnp.dot(normed_two.T, d_up, preferred_element_type=jnp.float32)
    d_normed_two = jnp.dot(d_gate, w_gate.T, preferred_element_type=jnp.float32) + jnp.dot(d_up, w_up.T, preferred_element_type=jnp.float32)
    grad_ffn_gain = lax.optimization_barrier(jnp.sum(d_normed_two * unit_two, axis=0))
    d_middle = upstream + norm_back(d_normed_two, unit_two, scale_two, ffn_gain)
    middle_b = rounded(d_middle)
    d_attn_f = jnp.dot(middle_b, w_out.T, preferred_element_type=jnp.float32)
    grad_out = jnp.dot(attn_b.T, middle_b, preferred_element_type=jnp.float32)
    d_attn = rounded(d_attn_f).astype(jnp.float32).reshape(length, HEADS, HEAD)
    attn_wide = attn_b.astype(jnp.float32).reshape(length, HEADS, HEAD)
    row_delta = lax.optimization_barrier(jnp.sum(d_attn * attn_wide, axis=-1))
    d_probs = jnp.einsum('qhd,khd->hqk', d_attn, v_wide)
    d_scores = attn_probs * (d_probs - row_delta.T[:, :, None])
    d_scores_b = rounded(d_scores).astype(jnp.float32)
    d_qrot = jnp.einsum('hqk,khd->qhd', d_scores_b, k_wide) * score_scale
    d_kwide = jnp.einsum('hqk,qhd->khd', d_scores_b, q_rot) * score_scale
    d_vwide = jnp.einsum('hqk,qhd->khd', probs_b, d_attn)
    d_krot = lax.optimization_barrier(jnp.sum(d_kwide.reshape(length, KV_HEADS, group_size, HEAD), axis=2))
    d_value = lax.optimization_barrier(jnp.sum(d_vwide.reshape(length, KV_HEADS, group_size, HEAD), axis=2))
    dq_turn = rotate(d_qrot, cosine, sine, -1.0)
    dk_turn = rotate(d_krot, cosine, sine, -1.0)
    grad_query_gain = lax.optimization_barrier(jnp.sum(dq_turn * q_unit, axis=(0, 1)))
    grad_key_gain = lax.optimization_barrier(jnp.sum(dk_turn * k_unit, axis=(0, 1)))
    d_query = norm_back(dq_turn, q_unit, q_scale, query_gain)
    d_key = norm_back(dk_turn, k_unit, k_scale, key_gain)
    dq_b = rounded(d_query.reshape(length, HEADS * HEAD))
    dk_b = rounded(d_key.reshape(length, KV_HEADS * HEAD))
    dv_b = rounded(d_value.reshape(length, KV_HEADS * HEAD))
    grad_query = jnp.dot(normed_one.T, dq_b, preferred_element_type=jnp.float32)
    grad_key = jnp.dot(normed_one.T, dk_b, preferred_element_type=jnp.float32)
    grad_value = jnp.dot(normed_one.T, dv_b, preferred_element_type=jnp.float32)
    d_normed_one = jnp.dot(dq_b, w_query.T, preferred_element_type=jnp.float32) + jnp.dot(dk_b, w_key.T, preferred_element_type=jnp.float32) + jnp.dot(dv_b, w_value.T, preferred_element_type=jnp.float32)
    grad_attn_gain = lax.optimization_barrier(jnp.sum(d_normed_one * unit_one, axis=0))
    in_grad = d_middle + norm_back(d_normed_one, unit_one, scale_one, attn_gain)
    grads = (grad_attn_gain, grad_query, grad_key, grad_value, grad_query_gain, grad_key_gain, grad_out, grad_ffn_gain, grad_gate, grad_up, grad_down)
    return (block_out, in_grad, grads)

def reference(block_in, out_grad, segment_ids, attn_gain, w_query, w_key, w_value, query_gain, key_gain, w_out, ffn_gain, w_gate, w_up, w_down):
    shapes = (attn_gain.shape, w_query.shape, w_key.shape, w_value.shape, query_gain.shape, key_gain.shape, w_out.shape, ffn_gain.shape, w_gate.shape, w_up.shape, w_down.shape)
    start_grads = tuple((jnp.zeros(shape_one, jnp.float32) for shape_one in shapes))

    def per_sequence(carried, items):
        stream, upstream, segments = items
        block_out, in_grad, grads = one_sequence(stream, upstream, segments, attn_gain, w_query, w_key, w_value, query_gain, key_gain, w_out, ffn_gain, w_gate, w_up, w_down)
        return (tuple((left + right for left, right in zip(carried, grads))), (block_out, in_grad))
    grads, (block_out, in_grad) = lax.scan(per_sequence, start_grads, (block_in, out_grad, segment_ids))
    return (block_out, in_grad, grads[0], grads[1], grads[2], grads[3], grads[4], grads[5], grads[6], grads[7], grads[8], grads[9], grads[10])
```

```python
import jax
import jax.numpy as jnp
from jax import lax
from jax.sharding import PartitionSpec as P

NORM_EPSILON = 1e-05
ROPE_BASE = 1000000.0
F32 = jnp.float32
BF16 = jnp.bfloat16


def rope_tables(length, head_width):
    half_width = head_width // 2
    exponents = jnp.arange(half_width, dtype=jnp.float32) * (2.0 / head_width)
    frequency = ROPE_BASE ** (-exponents)
    angles = jnp.arange(length, dtype=jnp.float32)[:, None] * frequency[None, :]
    return (jnp.cos(angles), jnp.sin(angles))


def rotate(vectors, cosine, sine, direction):
    half_width = vectors.shape[-1] // 2
    first_half = vectors[..., :half_width]
    second_half = vectors[..., half_width:]
    cos_rows = cosine[:, None, :]
    sin_rows = sine[:, None, :] * direction
    return jnp.concatenate(
        [
            first_half * cos_rows - second_half * sin_rows,
            second_half * cos_rows + first_half * sin_rows,
        ],
        axis=-1,
    )


def swap(values, axis, bit):
    count = lax.axis_size(axis)
    return lax.ppermute(values, axis, [(i, i ^ bit) for i in range(count)])


def bits_of(axis):
    count = lax.axis_size(axis)
    bits = []
    while count > 1:
        count //= 2
        bits.append(count)
    return bits


def row_order():
    order = [0]
    for bit in bits_of("row"):
        order = order + [j ^ bit for j in order]
    return order


def together(values):
    return lax.optimization_barrier(values)


def grow(block, axis, bit, dim):
    return jnp.concatenate([block, swap(block, axis, bit)], axis=dim)


def grow_both(one, one_step, two, two_step):
    got_one = swap(one, one_step[0], one_step[1])
    got_two = swap(two, two_step[0], two_step[1])
    got_one, got_two = together((got_one, got_two))
    return (
        jnp.concatenate([one, got_one], axis=one_step[2]),
        jnp.concatenate([two, got_two], axis=two_step[2]),
    )


def gather_all(block):
    col_steps = [("col", bit, 1) for bit in reversed(bits_of("col"))]
    row_steps = [("row", bit, 0) for bit in bits_of("row")]
    far, near = row_steps[:-1], row_steps[-1:]
    half = block.shape[0] // 2
    one, two = block[:half], block[half:]
    steps_one, steps_two = col_steps + far, far + col_steps
    for step_one, step_two in zip(steps_one, steps_two):
        one, two = grow_both(one, step_one, two, step_two)
    width = one.shape[1]
    full = jnp.concatenate(
        [one.reshape(-1, half, width), two.reshape(-1, half, width)], axis=1
    ).reshape(-1, width)
    for axis, bit, dim in near:
        full = grow(full, axis, bit, dim)
    return full


def halves(values, dim):
    middle = values.shape[dim] // 2
    if dim == 0:
        return values[:middle], values[middle:]
    return values[:, :middle], values[:, middle:]


def fold(values, axis, bit, dim):
    keep, give = halves(values, dim)
    return keep + swap(give.astype(BF16), axis, bit).astype(F32)


def fold_both(one, one_step, two, two_step):
    keep_one, give_one = halves(one, one_step[2])
    keep_two, give_two = halves(two, two_step[2])
    got_one = swap(give_one.astype(BF16), one_step[0], one_step[1])
    got_two = swap(give_two.astype(BF16), two_step[0], two_step[1])
    got_one, got_two = together((got_one, got_two))
    return keep_one + got_one.astype(F32), keep_two + got_two.astype(F32)


def scatter_all(terms):
    col_steps = [("col", bit, 1) for bit in bits_of("col")]
    row_steps = [("row", bit, 0) for bit in reversed(bits_of("row"))]
    near, far = row_steps[:1], row_steps[1:]
    for axis, bit, dim in near:
        terms = fold(terms, axis, bit, dim)
    rows = terms.shape[0] * len(near) * 2 // lax.axis_size("row")
    half, width = rows // 2, terms.shape[1]
    split = terms.reshape(-1, 2, half, width)
    one = split[:, 0].reshape(-1, width)
    two = split[:, 1].reshape(-1, width)
    steps_one, steps_two = far + col_steps, col_steps + far
    for step_one, step_two in zip(steps_one, steps_two):
        one, two = fold_both(one, step_one, two, step_two)
    return jnp.concatenate([one, two], axis=0)


def scatter_rows(terms):
    for bit in reversed(bits_of("row")):
        terms = fold(terms, "row", bit, 0)
    return terms


def col_gather(values, dim):
    for bit in reversed(bits_of("col")):
        values = grow(values, "col", bit, dim)
    return values


def col_total(values):
    for bit in bits_of("col"):
        values = values + swap(values, "col", bit)
    return values


def all_total(values, axes):
    for axis in axes:
        for bit in reversed(bits_of(axis)):
            values = values + swap(values, axis, bit)
    return values


def col_pieces(matrices, dim):
    count = lax.axis_size("col")
    index = lax.axis_index("col")
    pieces = []
    for offset in range(count):
        member = index ^ offset
        cut = []
        for matrix in matrices:
            width = matrix.shape[dim] // count
            cut.append(lax.dynamic_slice_in_dim(matrix, member * width, width, dim))
        pieces.append(jnp.concatenate(cut, axis=1) if len(cut) > 1 else cut[0])
    return pieces


def regroup(pieces, dim):
    got = [pieces[0]] + [
        swap(piece, "col", offset) for offset, piece in enumerate(pieces) if offset
    ]
    return jnp.concatenate(got, axis=dim)


def natural_cols(blocks, dim):
    index = lax.axis_index("col")
    count = len(blocks)
    stacked = jnp.stack(blocks)
    return jnp.concatenate(
        [
            lax.dynamic_index_in_dim(stacked, index ^ place, 0, keepdims=False)
            for place in range(count)
        ],
        axis=dim,
    )


def relative_rows(values, order):
    index = lax.axis_index("row")
    rows = values.shape[0] // len(order)
    return jnp.concatenate(
        [
            lax.dynamic_slice_in_dim(values, (index ^ offset) * rows, rows, 0)
            for offset in order
        ],
        axis=0,
    )


def contract_rows(left, right):
    return lax.dot_general(
        left, right, (((0,), (0,)), ((), ())), preferred_element_type=jnp.float32
    )


def times_transposed(left, right):
    return lax.dot_general(
        left, right, (((1,), (1,)), ((), ())), preferred_element_type=jnp.float32
    )


def times(left, right):
    return jnp.dot(left, right, preferred_element_type=jnp.float32)


def norm_back(grad_rows, unit_rows, scale_rows, gain, model_width):
    weighted = grad_rows * gain
    inner = col_total(jnp.sum(weighted * unit_rows, axis=1)) / model_width
    return scale_rows * (weighted - unit_rows * inner[:, None])


def head_norm_back(grad_rows, unit_rows, scale_rows, gain):
    weighted = grad_rows * gain
    return scale_rows * (
        weighted - unit_rows * jnp.mean(weighted * unit_rows, axis=-1, keepdims=True)
    )


def allowed_pairs(segments, positions, block_start, block_rows):
    rows = slice(block_start, block_start + block_rows)
    same_doc = segments[rows, None] == segments[None, :]
    causal = positions[rows, None] >= positions[None, :]
    return same_doc & causal


def attention_forward(q_rot, k_rot, v_rows, segments, positions, block_rows):
    length = q_rot.shape[0]
    score_scale = q_rot.shape[-1] ** (-0.5)
    outputs = []
    log_totals = []
    for block_start in range(0, length, block_rows):
        q_block = q_rot[block_start : block_start + block_rows]
        allowed = allowed_pairs(segments, positions, block_start, block_rows)
        scores = (
            jnp.einsum("qkgd,skd->kgqs", q_block, k_rot, preferred_element_type=jnp.float32)
            * score_scale
        )
        scores = jnp.where(allowed, scores, -jnp.inf)
        row_top = jnp.max(scores, axis=-1, keepdims=True)
        log_total = row_top + jnp.log(jnp.sum(jnp.exp(scores - row_top), axis=-1, keepdims=True))
        probs_b = jnp.exp(scores - log_total).astype(jnp.bfloat16)
        outputs.append(
            jnp.einsum("kgqs,skd->qkgd", probs_b, v_rows, preferred_element_type=jnp.float32)
        )
        log_totals.append(log_total)
    return (jnp.concatenate(outputs, axis=0), log_totals)


def attention_backward(q_rot, k_rot, v_rows, segments, positions, log_totals, d_attn, attn_b, block_rows):
    length = q_rot.shape[0]
    score_scale = q_rot.shape[-1] ** (-0.5)
    row_delta = jnp.sum(d_attn.astype(jnp.float32) * attn_b.astype(jnp.float32), axis=-1)
    query_parts = []
    d_krot = jnp.zeros(k_rot.shape, jnp.float32)
    d_value = jnp.zeros(v_rows.shape, jnp.float32)
    for block_index, block_start in enumerate(range(0, length, block_rows)):
        q_block = q_rot[block_start : block_start + block_rows]
        grad_block = d_attn[block_start : block_start + block_rows]
        allowed = allowed_pairs(segments, positions, block_start, block_rows)
        scores = (
            jnp.einsum("qkgd,skd->kgqs", q_block, k_rot, preferred_element_type=jnp.float32)
            * score_scale
        )
        attn_probs = jnp.exp(jnp.where(allowed, scores, -jnp.inf) - log_totals[block_index])
        probs_b = attn_probs.astype(jnp.bfloat16)
        d_probs = jnp.einsum(
            "qkgd,skd->kgqs", grad_block, v_rows, preferred_element_type=jnp.float32
        )
        delta_block = jnp.transpose(row_delta[block_start : block_start + block_rows], (1, 2, 0))[
            ..., None
        ]
        d_scores_b = (attn_probs * (d_probs - delta_block)).astype(jnp.bfloat16)
        query_parts.append(
            jnp.einsum("kgqs,skd->qkgd", d_scores_b, k_rot, preferred_element_type=jnp.float32)
            * score_scale
        )
        d_krot = (
            d_krot
            + jnp.einsum("kgqs,qkgd->skd", d_scores_b, q_block, preferred_element_type=jnp.float32)
            * score_scale
        )
        d_value = d_value + jnp.einsum(
            "kgqs,qkgd->skd", probs_b, grad_block, preferred_element_type=jnp.float32
        )
    return (jnp.concatenate(query_parts, axis=0), d_krot, d_value)


def body(
    block_in,
    out_grad,
    segment_ids,
    attn_gain,
    w_query,
    w_key,
    w_value,
    query_gain,
    key_gain,
    w_out,
    ffn_gain,
    w_gate,
    w_up,
    w_down,
):
    col_count = lax.axis_size("col")
    local_width = block_in.shape[2]
    model_width = local_width * col_count
    stream = block_in[0]
    upstream = out_grad[0]
    head_width = query_gain.shape[0]
    query_cols = w_query.shape[1] // col_count
    key_cols = w_key.shape[1] // col_count
    value_cols = w_value.shape[1] // col_count
    hidden_cols = w_gate.shape[1] // col_count
    key_heads = key_cols // head_width
    group_size = query_cols // key_cols
    order = row_order()

    scale_one = lax.rsqrt(col_total(jnp.sum(stream * stream, axis=1)) / model_width + NORM_EPSILON)[
        :, None
    ]
    unit_one = stream * scale_one
    normed_one = (unit_one * attn_gain).astype(BF16)
    rows_one = gather_all(normed_one)
    length = rows_one.shape[0]
    block_rows = min(512, length)

    qkv_pieces = col_pieces((w_query, w_key, w_value), 1)
    qkv_own = regroup(qkv_pieces, 0)
    qkv_local = jnp.concatenate(qkv_pieces, axis=1)
    out_pieces = col_pieces((w_out,), 0)
    out_own = regroup(out_pieces, 1)
    out_local = jnp.concatenate(out_pieces, axis=0)
    gate_own = regroup(col_pieces((w_gate, w_up), 1), 0)
    down_own = regroup(col_pieces((w_down,), 0), 1)
    grad_rows = gather_all(upstream.astype(BF16))

    segments = relative_rows(segment_ids[0], order)
    positions = relative_rows(jnp.arange(length, dtype=jnp.int32), order)
    cosine, sine = rope_tables(length, head_width)
    cosine, sine = relative_rows(cosine, order), relative_rows(sine, order)

    qkv = times(rows_one, qkv_own)
    query_rows = qkv[:, :query_cols].reshape(length, key_heads * group_size, head_width)
    key_rows = qkv[:, query_cols : query_cols + key_cols].reshape(length, key_heads, head_width)
    value_rows = qkv[:, query_cols + key_cols :].reshape(length, key_heads, head_width)
    q_scale = lax.rsqrt(jnp.mean(query_rows * query_rows, axis=-1, keepdims=True) + NORM_EPSILON)
    q_unit = query_rows * q_scale
    k_scale = lax.rsqrt(jnp.mean(key_rows * key_rows, axis=-1, keepdims=True) + NORM_EPSILON)
    k_unit = key_rows * k_scale
    q_rot = (
        rotate(q_unit * query_gain, cosine, sine, 1.0)
        .astype(BF16)
        .reshape(length, key_heads, group_size, head_width)
    )
    k_rot = rotate(k_unit * key_gain, cosine, sine, 1.0).astype(BF16)
    v_rows = value_rows.astype(BF16)
    attn_rows, log_totals = attention_forward(q_rot, k_rot, v_rows, segments, positions, block_rows)
    attn_b = attn_rows.astype(BF16)
    attn_cols = col_gather(attn_b.reshape(length, query_cols), 1)
    middle = stream + scatter_rows(times(attn_cols, out_local))
    scale_two = lax.rsqrt(col_total(jnp.sum(middle * middle, axis=1)) / model_width + NORM_EPSILON)[
        :, None
    ]
    unit_two = middle * scale_two
    normed_two = (unit_two * ffn_gain).astype(BF16)
    rows_two = gather_all(normed_two)
    gate_up = times(rows_two, gate_own)
    gate = gate_up[:, :hidden_cols]
    up_proj = gate_up[:, hidden_cols:]
    sigmoid_gate = jax.nn.sigmoid(gate)
    silu_gate = gate * sigmoid_gate
    activated = (silu_gate * up_proj).astype(BF16)
    d_act = times_transposed(grad_rows, down_own)
    d_gate = d_act * up_proj * (sigmoid_gate * (1.0 + gate * (1.0 - sigmoid_gate)))
    d_up = d_act * silu_gate
    d_gate_up = jnp.concatenate([d_gate, d_up], axis=1).astype(BF16)

    down_terms = contract_rows(activated, grad_rows).astype(BF16)
    gate_terms = jnp.concatenate(
        [
            contract_rows(rows_two[:, k * local_width : (k + 1) * local_width], d_gate_up)
            for k in range(col_count)
        ],
        axis=1,
    ).astype(BF16)
    down_part = lax.psum_scatter(down_terms, "dp", scatter_dimension=0, tiled=True)
    gate_part = lax.psum_scatter(gate_terms, "dp", scatter_dimension=0, tiled=True)

    d_normed_two = scatter_all(times_transposed(d_gate_up, gate_own))
    gain_two = jnp.sum(d_normed_two * unit_two, axis=0)
    d_middle = upstream + norm_back(d_normed_two, unit_two, scale_two, ffn_gain, model_width)
    middle_b = d_middle.astype(BF16)
    middle_rows = gather_all(middle_b)
    block_out = middle + scatter_all(times(activated, down_own))

    def back_to_rows(part, width):
        pieces = [part[:, k * width : (k + 1) * width] for k in range(col_count)]
        got = [pieces[0]] + [
            swap(piece, "col", offset) for offset, piece in enumerate(pieces) if offset
        ]
        whole = lax.all_gather(jnp.concatenate(got, axis=1), "dp", axis=0, tiled=True)
        return [whole[:, k * width : (k + 1) * width] for k in range(col_count)]

    down_blocks = back_to_rows(down_part, local_width)
    gate_blocks = back_to_rows(gate_part, 2 * hidden_cols)
    grad_down = natural_cols(down_blocks, 0).astype(F32)
    grad_gate = natural_cols([block[:, :hidden_cols] for block in gate_blocks], 1).astype(F32)
    grad_up = natural_cols([block[:, hidden_cols:] for block in gate_blocks], 1).astype(F32)

    d_attn_f = times_transposed(middle_rows, out_own)
    out_terms = contract_rows(attn_cols, middle_rows[:, :local_width]).astype(BF16)
    d_attn = d_attn_f.astype(BF16).reshape(length, key_heads, group_size, head_width)
    d_qrot, d_krot, d_value = attention_backward(
        q_rot, k_rot, v_rows, segments, positions, log_totals, d_attn, attn_b, block_rows
    )
    dq_turn = rotate(d_qrot.reshape(length, key_heads * group_size, head_width), cosine, sine, -1.0)
    dk_turn = rotate(d_krot, cosine, sine, -1.0)
    query_gain_part = jnp.sum(dq_turn * q_unit, axis=(0, 1))
    key_gain_part = jnp.sum(dk_turn * k_unit, axis=(0, 1))
    d_query = head_norm_back(dq_turn, q_unit, q_scale, query_gain)
    d_key = head_norm_back(dk_turn, k_unit, k_scale, key_gain)
    d_qkv = jnp.concatenate(
        [
            d_query.reshape(length, query_cols),
            d_key.reshape(length, key_cols),
            d_value.reshape(length, value_cols),
        ],
        axis=1,
    ).astype(BF16)
    d_qkv_cols = col_gather(d_qkv, 1)
    qkv_terms = contract_rows(rows_one[:, :local_width], d_qkv_cols).astype(BF16)
    qkv_sum, out_sum = lax.psum((qkv_terms, out_terms), "dp")
    own_cols = query_cols + key_cols + value_cols
    qkv_blocks = [qkv_sum[:, k * own_cols : (k + 1) * own_cols] for k in range(col_count)]
    grad_query = natural_cols([b[:, :query_cols] for b in qkv_blocks], 1).astype(F32)
    grad_key = natural_cols(
        [b[:, query_cols : query_cols + key_cols] for b in qkv_blocks], 1
    ).astype(F32)
    grad_value = natural_cols([b[:, query_cols + key_cols :] for b in qkv_blocks], 1).astype(F32)
    grad_out = natural_cols(
        [out_sum[k * query_cols : (k + 1) * query_cols] for k in range(col_count)], 0
    ).astype(F32)

    d_normed_one = scatter_rows(times_transposed(d_qkv_cols, qkv_local))
    gain_one = jnp.sum(d_normed_one * unit_one, axis=0)
    in_grad = d_middle + norm_back(d_normed_one, unit_one, scale_one, attn_gain, model_width)

    gain_sums = all_total(
        jnp.concatenate([gain_one, gain_two, query_gain_part, key_gain_part]), ("row", "dp")
    )
    grad_attn_gain = gain_sums[:local_width]
    grad_ffn_gain = gain_sums[local_width : 2 * local_width]
    head_gains = all_total(gain_sums[2 * local_width :], ("col",))
    grad_query_gain = head_gains[:head_width]
    grad_key_gain = head_gains[head_width:]
    return (
        block_out[None],
        in_grad[None],
        grad_attn_gain,
        grad_query,
        grad_key,
        grad_value,
        grad_query_gain,
        grad_key_gain,
        grad_out,
        grad_ffn_gain,
        grad_gate,
        grad_up,
        grad_down,
    )


def solution(mesh):
    placed = (
        P("dp", "row", "col"),
        P("dp", "row", "col"),
        P("dp", None),
        P("col"),
        P("col", "row"),
        P("col", "row"),
        P("col", "row"),
        P(),
        P(),
        P("row", "col"),
        P("col"),
        P("col", "row"),
        P("col", "row"),
        P("row", "col"),
    )
    return jax.shard_map(
        body,
        mesh=mesh,
        in_specs=placed,
        out_specs=(
            P("dp", "row", "col"),
            P("dp", "row", "col"),
            P("col"),
            P("col", "row"),
            P("col", "row"),
            P("col", "row"),
            P(),
            P(),
            P("row", "col"),
            P("col"),
            P("col", "row"),
            P("col", "row"),
            P("row", "col"),
        ),
        check_vma=False,
    )
```
